128 devices in a mesh: body: 2 (over core), sub: 64 (over x, y, z).
Axes of the slice: x: 4, y: 4, z: 4, core: 2. Of those that a mesh axis runs over, the one named last changes fastest.
Arguments:
- rhs: float32 [8, 4096, 256], P(None, 'sub'), may hold values from -50 to 50
- compliance: float32 [4096, 256], P('sub'), may hold values from 0.5 to 2
- plate_owner: int32 [4096, 1], P('sub'), may hold values from 0 to 63; in each aligned block of 64 rows (0 to 63, 64 to 127, ...) at most 2 rows name the same one
- found_owner: int32 [4096, 1], P('sub'), may hold values from 0 to 63; in each aligned block of 64 rows (0 to 63, 64 to 127, ...) at most 2 rows name the same one
- slot_pairs: int32 [4096, 2], P('sub'), may hold values from 0 to 7
- active: int32 [4096], P('sub'), may hold values 0 or 1
- inverse: bfloat16 [2, 64, 2048, 2048], P('body', 'sub'), may hold values from -0.06 to 4, as said below
Outputs:
- multipliers: float32 [8, 4096, 256], P(None, 'sub')
The draws below stay inside these ranges and needn't reach their ends.
Inputs may be any that keep to these rules, and one draw needn't show every extreme that they name: `plate_owner`: at most 2 patches among the list of one index of sub name the same plate substructure; some list names one exactly 2 times. `found_owner`: at most 2 patches among the list of one index of sub name the same foundation substructure; some list names one exactly 2 times. Each block inverse[b, t] is symmetric positive definite.
All inputs are finite; a program needn't handle non-finite values. No bound on the sum of `active` on one device may be relied on, other than what follows from the above.
Results may differ from the reference program's by a relative error of at most 0.0055.
Values sent between devices are 32-bit elements; how exact they have to be, the bound alone decides.
A program may use at most 64 MiB of HBM per device.

```python
import math
import jax
import jax.numpy as jnp
import numpy as np
from jax import lax

GAP = 256
SLOTS = 8
CASES = 8
ITERS = 4
PATCH_DEV = 64
PATCHES = 4096
CAP = 2
IFACE = 2048
N_SUB = 64


def draw_inverse(key, part):
    keys = jax.random.split(key, 2 * N_SUB)
    index = jnp.arange(IFACE, dtype=jnp.int32)
    reach = 0.06 / (1.0 + jnp.abs(index[:, None] - index[None, :]).astype(jnp.float32))
    diagonal_mask = index[:, None] == index[None, :]

    def one_block(block_key):
        first, second = jax.random.split(block_key)
        rough = 0.3 + 0.7 * jax.random.uniform(first, (IFACE, IFACE), jnp.float32, -1.0, 1.0)
        middle = jnp.exp(jax.random.uniform(second, (IFACE,), jnp.float32, 0.0, math.log(2.0)))
        symmetric = 0.5 * (rough + rough.T) * reach
        return jnp.where(diagonal_mask, middle[None, :], symmetric).astype(jnp.bfloat16)
    return lax.map(one_block, keys).reshape(2, N_SUB, IFACE, IFACE)


def draw_rhs(key, part):
    first, second = jax.random.split(key, 2)
    rising = jnp.exp(math.log(10.0) * jnp.arange(PATCHES).astype(jnp.float32) / max(PATCHES - 1, 1))
    case_scale = jnp.exp(math.log(10.0) * jax.random.uniform(second, (CASES,), jnp.float32))
    base = jnp.clip(jax.random.normal(first, (CASES, PATCHES, GAP), jnp.float32), -5.0, 5.0)
    return base * rising[None, :, None] * case_scale[:, None, None] / 10.0


def set_ends(values, rng, low, largest):
    shape = values.shape
    place = [jax.random.randint(jax.random.fold_in(rng, axis), (), 0, shape[axis]) for axis in range(len(shape))]
    values = values.at[tuple(place)].set(low)
    longest = shape.index(max(shape))
    place[longest] = (place[longest] + 1) % shape[longest]
    return values.at[tuple(place)].set(largest)


def block_levels(own_key, shape, cuts, smallest, largest):
    factor_of, own = 1.0, jax.random.fold_in(own_key, 6)
    for axis_at, shards_of in cuts:
        draws = jnp.exp(jax.random.uniform(jax.random.fold_in(own, axis_at), (shards_of,), jnp.float32, smallest / len(cuts), largest / len(cuts)))
        factor_of = factor_of * jnp.repeat(draws, shape[axis_at] // shards_of).reshape([-1 if axis == axis_at else 1 for axis in range(len(shape))])
    return factor_of


def routed_block(key, own, number, rows, number_of, top, most, lean):
    sequence = jax.random.permutation(key, number_of)
    heavy_load, common = load_shares(number_of, rows * top, most, lean, True), load_shares(number_of, rows * top, most, lean, False)
    places = jnp.arange(number_of)

    def named(sizes, turn):
        used = int((sizes > 0).sum())
        fixed = max(1, used // 4)
        shifted = fixed + (places - fixed + turn * (used - fixed)) % max(1, number_of - fixed)
        return jnp.zeros((number_of,), jnp.int32).at[sequence[jnp.where(places < fixed, places, shifted)]].set(jnp.asarray(sizes, jnp.int32))

    sizes = jnp.where(number % 4 == 0, named(heavy_load, number // 4), named(common, number - number // 4 - 1))
    mixed = jax.random.permutation(jax.random.fold_in(own, 3), number_of)
    donor, taker = mixed[0:number_of // 2 * 2:2], mixed[1:number_of // 2 * 2:2]
    slack = jnp.minimum(sizes[donor] - 1, most - sizes[taker]) // 2
    slack = jnp.where((donor == sequence[0]) | (taker == sequence[0]) | (sizes[taker] == 0), 0, jnp.maximum(slack, 0))
    shifted = jax.random.randint(jax.random.fold_in(own, 4), (number_of // 2,), 0, 1 << 20) % (slack + 1)
    sizes = sizes.at[donor].add(-shifted).at[taker].add(shifted)
    members = jnp.searchsorted(jnp.cumsum(sizes), jnp.arange(rows * top), side="right").astype(jnp.int32)
    listing = members.reshape(top, rows).T
    listing = listing[jax.random.permutation(jax.random.fold_in(own, 1), rows)]
    turn = jax.random.randint(jax.random.fold_in(own, 2), (rows, 1), 0, top)
    return jnp.take_along_axis(listing, (jnp.arange(top)[None, :] + turn) % top, axis=1)


def load_shares(amount, total, limit, lean, full):
    loads = [(1 << 20) // math.isqrt(grade ** lean) + 1 for grade in range(1, amount + 1)]
    largest = limit if full else min(limit, max(-(-total // amount), total * loads[0] // sum(loads)))
    least = 1 if total - largest >= amount - 1 else 0
    holding, surplus = [largest] + [least] * (amount - 1), total - largest - least * (amount - 1)
    while surplus > 0:
        candidates = [i for i in range(1, amount) if holding[i] < largest] or [i for i in range(1, amount) if holding[i] < limit]
        whole, left = sum([loads[i] for i in candidates]), surplus
        for i in candidates:
            addition = min(limit - holding[i], max(1, left * loads[i] // whole), surplus)
            holding[i] = holding[i] + addition
            surplus = surplus - addition
    return np.array(holding)


def setup_inputs(seed: int = 0) -> dict:
    key_list = jax.random.split(jax.random.key(seed), 8)
    rhs = draw_rhs(jax.random.fold_in(key_list[7], 71), 0)
    compliance = jnp.clip(jnp.exp(math.log(2.0) - 1.3862944 * jax.random.uniform(key_list[1], (PATCHES, GAP), jnp.float32) ** block_levels(key_list[1], (PATCHES, GAP), ((0, 64),), -0.2, 0.2)), 0.5, 2.0)
    plate_owner_keys = jax.random.split(jax.random.fold_in(key_list[2], 1), PATCHES // PATCH_DEV)
    plate_owner_turns = jax.random.permutation(jax.random.fold_in(key_list[2], 3), PATCHES // PATCH_DEV)
    plate_owner = jax.vmap(lambda own, number: routed_block(jax.random.fold_in(key_list[2], 2), own, number, PATCH_DEV, N_SUB, 1, CAP, 2))(plate_owner_keys, plate_owner_turns).reshape((PATCHES, 1))
    found_owner_keys = jax.random.split(jax.random.fold_in(key_list[3], 1), PATCHES // PATCH_DEV)
    found_owner_turns = jax.random.permutation(jax.random.fold_in(key_list[3], 3), PATCHES // PATCH_DEV)
    found_owner = jax.vmap(lambda own, number: routed_block(jax.random.fold_in(key_list[3], 2), own, number, PATCH_DEV, N_SUB, 1, CAP, 3))(found_owner_keys, found_owner_turns).reshape((PATCHES, 1))
    slot_pairs = set_ends(jax.random.randint(key_list[4], (PATCHES, 2), 0, SLOTS), jax.random.fold_in(key_list[4], 1), 0, SLOTS - 1).astype(jnp.int32)
    active = set_ends((jax.random.randint(key_list[5], (PATCHES,), 0, 4) < 3).astype(jnp.int32), jax.random.fold_in(key_list[5], 1), 0, 1)
    inverse = draw_inverse(jax.random.fold_in(key_list[7], 71), 0)
    return dict(rhs=rhs, compliance=compliance, plate_owner=plate_owner, found_owner=found_owner, slot_pairs=slot_pairs, active=active, inverse=inverse)


def interface_response(field, owner, slot, block_list):
    rows = jnp.transpose(field, (1, 0, 2))
    target = (owner * SLOTS + slot).astype(jnp.int32)
    summed = jax.ops.segment_sum(rows, target, num_segments=N_SUB * SLOTS)
    summed = summed.reshape(N_SUB, SLOTS, CASES, GAP).transpose(0, 2, 1, 3).reshape(N_SUB, CASES, SLOTS * GAP)
    load_vectors = summed.astype(jnp.bfloat16)

    def apply_block(pair):
        return jnp.dot(pair[0], pair[1], preferred_element_type=jnp.float32)

    response = lax.map(apply_block, (load_vectors, block_list))
    response = response.reshape(N_SUB, CASES, SLOTS, GAP)
    picked = response[owner, :, slot, :]
    return jnp.transpose(picked, (1, 0, 2))


def reference(rhs, compliance, plate_owner, found_owner, slot_pairs, active, inverse):
    keep = active.astype(jnp.float32)[None, :, None]
    owners = (plate_owner[:, 0], found_owner[:, 0])

    def operate(field):
        total = jnp.zeros_like(field)
        for side in range(2):
            total = total + interface_response(field, owners[side], slot_pairs[:, side], inverse[side])
        return keep * (total + compliance[None] * field)

    def products(left, right):
        return jnp.sum(left * right, axis=(1, 2))

    residual = keep * rhs
    solution = jnp.zeros_like(rhs)
    direction = residual
    norm_now = products(residual, residual)
    for step in range(ITERS):
        image = operate(direction)
        alpha = norm_now / products(direction, image)
        solution = solution + alpha[:, None, None] * direction
        residual = residual - alpha[:, None, None] * image
        norm_next = products(residual, residual)
        direction = residual + (norm_next / norm_now)[:, None, None] * direction
        norm_now = norm_next
    return solution
```

```python
import functools
import jax
import jax.numpy as jnp
from jax import lax
from jax.experimental import pallas as pl
from jax.experimental.pallas import tpu as pltpu
from jax.sharding import PartitionSpec as P

ITERS = 4
GROUPS = 2
ROOM = 2
UNROLL = 8
MESH = pl.DeviceIdType.MESH
FWD_SEND, FWD_RECV, RET_SEND, RET_RECV, FS_SEND, FS_RECV, RS_SEND, RS_RECV = range(8)


def to_row(col):
    lane = lax.broadcasted_iota(jnp.int32, (8, 128), 1)
    sub = lax.broadcasted_iota(jnp.int32, (8, 128), 0)
    spread = jnp.where(lane == sub, jnp.broadcast_to(col, (8, 128)), 0.0)
    return jnp.sum(spread, axis=0, keepdims=True)


def to_col(row):
    lane = lax.broadcasted_iota(jnp.int32, (8, 128), 1)
    sub = lax.broadcasted_iota(jnp.int32, (8, 128), 0)
    spread = jnp.where(lane == sub, jnp.broadcast_to(row, (8, 128)), 0.0)
    return jnp.sum(spread, axis=1, keepdims=True)


def wait_bytes(ref, sem):
    pltpu.make_async_copy(ref, ref, sem).wait()


def kernel(
    nsub, npatch, nslot, width,
    src, own, rank, keep, rhs, comp, slots, inv_hbm, out,
    inv, res, dirn, sol, fsend, frecv, rsend, rrecv0, rrecv1, psend, precv,
    load, lhs, resp, slot_in, slot_sm, slot_vec, fsc, fsc_in, rsc, rsc_in,
    sems, psem_send, psem_recv, slot_send, slot_recv, misc,
):
    rrecv = (rrecv0, rrecv1)
    b = lax.axis_index("body")
    me = lax.axis_index("sub")
    tile = (8, width)
    top = lax.broadcasted_iota(jnp.int32, tile, 0) < 4
    half = npatch // 2

    def swap(v):
        return pltpu.roll(v, 4, 0)

    def peer(i):
        return lax.rem(me + i, nsub)

    def remote(src_ref, dst_ref, send, recv, p):
        return pltpu.make_async_remote_copy(
            src_ref=src_ref, dst_ref=dst_ref, send_sem=send, recv_sem=recv,
            device_id=(b, p), device_id_type=MESH,
        )

    barrier = pltpu.get_barrier_semaphore()

    def greet(i, c):
        pl.semaphore_signal(barrier, inc=1, device_id=(b, peer(i)), device_id_type=MESH)
        return c

    lax.fori_loop(1, nsub, greet, 0)
    pl.semaphore_signal(barrier, inc=1, device_id=(1 - b, me), device_id_type=MESH)

    inv_copy = pltpu.make_async_copy(inv_hbm, inv, misc)
    inv_copy.start()

    def start_residual(i, accs):
        accs = list(accs)
        for u in range(UNROLL):
            p = i * UNROLL + u
            v = rhs[p]
            w = swap(v)
            for g in range(GROUPS):
                t = jnp.where(top, v, w) if g == 0 else jnp.where(top, w, v)
                res[g, p] = t
                dirn[g, p] = jnp.zeros(tile, jnp.float32)
                sol[g, p] = jnp.zeros(tile, jnp.float32)
                accs[g] = accs[g] + t * t
        return tuple(accs)

    zero = jnp.zeros(tile, jnp.float32)
    accs = lax.fori_loop(0, npatch // UNROLL, start_residual, (zero,) * GROUPS)
    for g in range(GROUPS):
        for s in range(nslot):
            load[g, s] = zero

    pl.semaphore_wait(barrier, nsub)

    def send_slots(i, c):
        p = peer(i)
        remote(slots.at[p], slot_in.at[me], slot_send, slot_recv, p).start()
        return c

    lax.fori_loop(1, nsub, send_slots, 0)
    pltpu.make_async_copy(slots.at[me], slot_in.at[me], slot_recv).start()

    def pack_forward(g, t):
        a = res[g, src[t * ROOM]]
        z = res[g, src[t * ROOM + 1]]
        fsend[g, t] = jnp.where(top, a, z)

    def forward(g, acc):
        fsc[g] = to_row(jnp.sum(acc, axis=1, keepdims=True))

        def one(i, c):
            p = peer(i)
            pack_forward(g, p)
            remote(fsend.at[g, p], frecv.at[g, me], sems.at[FWD_SEND, g], sems.at[FWD_RECV, g], p).start()
            remote(fsc.at[g], fsc_in.at[g, me], sems.at[FS_SEND, g], sems.at[FS_RECV, g], p).start()
            return c

        lax.fori_loop(1, nsub, one, 0)
        pack_forward(g, me)
        pltpu.make_async_copy(fsend.at[g, me], frecv.at[g, me], sems.at[FWD_RECV, g]).start()
        pltpu.make_async_copy(fsc.at[g], fsc_in.at[g, me], sems.at[FS_RECV, g]).start()

    def receive_forward(g, rr):
        wait_bytes(frecv.at[g], sems.at[FWD_RECV, g])
        wait_bytes(fsc_in.at[g], sems.at[FS_RECV, g])
        wait_bytes(fsend.at[g, pl.ds(0, nsub - 1)], sems.at[FWD_SEND, g])
        wait_bytes(fsc_in.at[g, pl.ds(0, nsub - 1)], sems.at[FS_SEND, g])
        new = to_col(jnp.sum(fsc_in[g], axis=0))
        beta = jnp.broadcast_to(new / rr, tile)

        def gather(i, accs):
            accs = list(accs)
            for u in range(4):
                s = i * 4 + u
                v = frecv[g, s]
                which = slot_vec[s]
                for k in range(nslot):
                    accs[k] = accs[k] + jnp.where(which == k, v, 0.0)
            return tuple(accs)

        sums = lax.fori_loop(0, nsub // 4, gather, (zero,) * nslot)
        for k in range(nslot):
            v = sums[k]
            v = v + swap(v) + beta * load[g, k]
            load[g, k] = v
            high = v.astype(jnp.bfloat16).astype(jnp.float32)
            lhs[:, k * width:(k + 1) * width] = jnp.where(top, high, v - high).astype(jnp.bfloat16)

        def column(n, acc):
            cols = pl.ds(pl.multiple_of(n * width, width), width)
            o = jnp.dot(lhs[...], inv[:, cols], preferred_element_type=jnp.float32)
            o = o + swap(o)
            resp[n] = o
            return acc + load[g, n] * o

        acc = lax.fori_loop(0, nslot, column, zero)

        def turn(i, acc):
            rows = comp[pl.ds(pl.multiple_of(i * UNROLL, UNROLL), UNROLL), :]
            for u in range(UNROLL):
                p = i * UNROLL + u
                v = res[g, p] + beta * dirn[g, p]
                dirn[g, p] = v
                acc = acc + rows[u:u + 1, :] * (v * v)
            return acc

        acc2 = lax.fori_loop(0, npatch // UNROLL, turn, zero)
        acc = acc + jnp.where(b == 0, 1.0, 0.0) * acc2
        return new, acc

    def pack_return(g, s):
        a = resp[jnp.maximum(slot_sm[s, 0, 0], 0)]
        z = resp[jnp.maximum(slot_sm[s, 0, 1], 0)]
        rsend[g, s] = jnp.where(top, a, z)

    def send_back(g, acc, data):
        rsc[g] = to_row(jnp.sum(acc, axis=1, keepdims=True))

        def one(i, c):
            p = peer(i)
            if data:
                pack_return(g, p)
                remote(rsend.at[g, p], rrecv[g].at[me], sems.at[RET_SEND, g], sems.at[RET_RECV, g], p).start()
            remote(rsc.at[g], rsc_in.at[g, me], sems.at[RS_SEND, g], sems.at[RS_RECV, g], p).start()
            return c

        lax.fori_loop(1, nsub, one, 0)
        if data:
            pack_return(g, me)
            pltpu.make_async_copy(rsend.at[g, me], rrecv[g].at[me], sems.at[RET_RECV, g]).start()
        pltpu.make_async_copy(rsc.at[g], rsc_in.at[g, me], sems.at[RS_RECV, g]).start()

    def partner(g, par, first):
        span = pl.ds(first, half + 1 - first)
        return pltpu.make_async_remote_copy(
            src_ref=psend.at[g, span], dst_ref=precv.at[par, g, span],
            send_sem=psem_send.at[g], recv_sem=psem_recv.at[par, g],
            device_id=(1 - b, me), device_id_type=MESH,
        )

    def receive_scalars(g):
        wait_bytes(rsc_in.at[g], sems.at[RS_RECV, g])
        wait_bytes(rsc_in.at[g, pl.ds(0, nsub - 1)], sems.at[RS_SEND, g])
        part = jnp.broadcast_to(to_col(jnp.sum(rsc_in[g], axis=0)), tile)
        psend[g, half] = part
        return part

    def receive_return(g, par, rr):
        wait_bytes(rrecv[g], sems.at[RET_RECV, g])
        wait_bytes(rsend.at[g, pl.ds(0, nsub - 1)], sems.at[RET_SEND, g])
        part = receive_scalars(g)

        def pick(i, c):
            for u in range(4):
                p = i * 4 + u
                q = p + half
                a = rrecv[g][own[p]]
                z = rrecv[g][own[q]]
                a = jnp.where(rank[p] == 0, a, swap(a))
                z = jnp.where(rank[q] == 0, swap(z), z)
                psend[g, p] = jnp.where(top, a, z)
            return c

        lax.fori_loop(0, half // 4, pick, 0)
        copy = partner(g, par, 0)
        copy.start()
        copy.wait()
        alpha = rr / (part + precv[par, g, half])

        def update(i, acc):
            low = comp[pl.ds(pl.multiple_of(i * UNROLL, UNROLL), UNROLL), :]
            high = comp[pl.ds(pl.multiple_of(half + i * UNROLL, UNROLL), UNROLL), :]
            for u in range(UNROLL):
                p = i * UNROLL + u
                pair = psend[g, p] + precv[par, g, p]
                other = swap(pair)
                for rows, q, v in (
                    (low, p, jnp.where(top, pair, other)),
                    (high, p + half, jnp.where(top, other, pair)),
                ):
                    d = dirn[g, q]
                    image = keep[q] * v + rows[u:u + 1, :] * d
                    sol[g, q] = sol[g, q] + alpha * d
                    r = res[g, q] - alpha * image
                    res[g, q] = r
                    acc = acc + r * r
            return acc

        return lax.fori_loop(0, half // UNROLL, update, zero)

    for g in range(GROUPS):
        forward(g, accs[g])

    wait_bytes(slot_in, slot_recv)
    wait_bytes(slot_in.at[pl.ds(0, nsub - 1)], slot_send)
    slot_copy = pltpu.make_async_copy(slot_in, slot_sm, misc)
    inv_copy.wait()
    slot_copy.start()
    slot_copy.wait()

    def spread_slots(i, c):
        for u in range(4):
            s = i * 4 + u
            slot_vec[s] = jnp.where(top, slot_sm[s, 0, 0], slot_sm[s, 0, 1])
        return c

    lax.fori_loop(0, nsub // 4, spread_slots, 0)

    def iteration(k, rrs):
        rrs = list(rrs)
        for g in range(GROUPS):
            rrs[g], acc = receive_forward(g, rrs[g])
            send_back(g, acc, True)
        for g in range(GROUPS):
            acc = receive_return(g, lax.rem(k, 2), jnp.broadcast_to(rrs[g], tile))
            forward(g, acc)
        return tuple(rrs)

    one = jnp.ones((8, 1), jnp.float32)
    rrs = list(lax.fori_loop(0, ITERS - 1, iteration, (one,) * GROUPS))
    par = (ITERS - 1) % 2
    for g in range(GROUPS):
        rrs[g], acc = receive_forward(g, rrs[g])
        send_back(g, acc, False)
    alphas = []
    for g in range(GROUPS):
        part = receive_scalars(g)
        copy = partner(g, par, half)
        copy.start()
        copy.wait()
        alphas.append(jnp.broadcast_to(rrs[g], tile) / (part + precv[par, g, half]))

    def finish(i, c):
        for u in range(UNROLL):
            p = i * UNROLL + u
            a = sol[0, p] + alphas[0] * dirn[0, p]
            z = sol[1, p] + alphas[1] * dirn[1, p]
            out[p] = jnp.where(top, a, z)
        return c

    lax.fori_loop(0, npatch // UNROLL, finish, 0)


def on_device(nsub, rhs, compliance, plate_owner, found_owner, slot_pairs, active, inverse):
    side = lax.axis_index("body")
    ncase, npatch, width = rhs.shape
    iface = inverse.shape[-1]
    nslot = iface // width
    nrow = nsub * ROOM
    owner = jnp.where(side == 0, plate_owner[:, 0], found_owner[:, 0])
    slot = jnp.where(side == 0, slot_pairs[:, 0], slot_pairs[:, 1])
    patch = jnp.arange(npatch, dtype=jnp.int32)
    same = (patch[None, :] < patch[:, None]) & (owner[None, :] == owner[:, None])
    rank = jnp.sum(same.astype(jnp.int32), axis=1)
    placed = (owner * ROOM + rank)[None, :] == jnp.arange(nrow, dtype=jnp.int32)[:, None]
    source = jnp.sum(jnp.where(placed, patch[None, :], 0), axis=1)
    sent_slot = jnp.sum(jnp.where(placed, slot[None, :] + 1, 0), axis=1) - 1
    slots = jnp.pad(sent_slot.reshape(nsub, 1, ROOM), ((0, 0), (0, 0), (0, 128 - ROOM)))
    keep = active.astype(jnp.float32)
    masked = jnp.transpose(keep[None, :, None] * rhs, (1, 0, 2))
    comp = keep[:, None] * compliance

    f32, i32 = jnp.float32, jnp.int32
    vmem = pl.BlockSpec(memory_space=pltpu.VMEM)
    smem = pl.BlockSpec(memory_space=pltpu.SMEM)
    state = pltpu.VMEM((GROUPS, npatch, 8, width), f32)
    message = pltpu.VMEM((GROUPS, nsub, 8, width), f32)
    single = pltpu.VMEM((nsub, 8, width), f32)
    half = npatch // 2
    result = pl.pallas_call(
        functools.partial(kernel, nsub, npatch, nslot, width),
        out_shape=jax.ShapeDtypeStruct((npatch, ncase, width), f32),
        in_specs=[smem, smem, smem, smem, vmem, vmem, vmem, pl.BlockSpec(memory_space=pl.ANY)],
        out_specs=vmem,
        scratch_shapes=[
            pltpu.VMEM((iface, iface), jnp.bfloat16),
            state, state, state, message, message, message, single, single,
            pltpu.VMEM((GROUPS, half + 1, 8, width), f32),
            pltpu.VMEM((2, GROUPS, half + 1, 8, width), f32),
            pltpu.VMEM((GROUPS, nslot, 8, width), f32),
            pltpu.VMEM((8, iface), jnp.bfloat16),
            pltpu.VMEM((nslot, 8, width), f32),
            pltpu.VMEM((nsub, 1, 128), i32),
            pltpu.SMEM((nsub, 1, 128), i32),
            pltpu.VMEM((nsub, 8, width), i32),
            pltpu.VMEM((GROUPS, 1, 128), f32),
            pltpu.VMEM((GROUPS, nsub, 1, 128), f32),
            pltpu.VMEM((GROUPS, 1, 128), f32),
            pltpu.VMEM((GROUPS, nsub, 1, 128), f32),
            pltpu.SemaphoreType.DMA((8, GROUPS)),
            pltpu.SemaphoreType.DMA((GROUPS,)),
            pltpu.SemaphoreType.DMA((2, GROUPS)),
            pltpu.SemaphoreType.DMA,
            pltpu.SemaphoreType.DMA,
            pltpu.SemaphoreType.DMA,
        ],
        compiler_params=pltpu.CompilerParams(
            collective_id=0, has_side_effects=True, vmem_limit_bytes=48 * 2**20
        ),
    )(source, owner, rank, keep, masked, comp, slots, inverse[0, 0])
    return jnp.transpose(result, (1, 0, 2))


def solution(mesh):
    in_specs = (
        P(None, "sub", None),
        P("sub", None),
        P("sub", None),
        P("sub", None),
        P("sub", None),
        P("sub"),
        P("body", "sub", None, None),
    )
    return jax.shard_map(
        functools.partial(on_device, mesh.shape["sub"]),
        mesh=mesh, in_specs=in_specs, out_specs=P(None, "sub", None), check_vma=False,
    )
```

```python
import functools
import jax
import jax.numpy as jnp
from jax import lax
from jax.experimental import pallas as pl
from jax.experimental.pallas import tpu as pltpu
from jax.sharding import PartitionSpec as P

ITERS = 4
GROUPS = 2
ROOM = 2
UNROLL = 8
ISSUE = 9
SPAN = 8
MESH = pl.DeviceIdType.MESH
FWD_SEND, FWD_RECV, RET_SEND, RET_RECV = range(4)
NEAR_SEND, NEAR_RECV, FAR_SEND, FAR_RECV, ALL_SEND, ALL_RECV = range(4, 10)


def to_row(col):
    lane = lax.broadcasted_iota(jnp.int32, (8, 128), 1)
    sub = lax.broadcasted_iota(jnp.int32, (8, 128), 0)
    spread = jnp.where(lane == sub, jnp.broadcast_to(col, (8, 128)), 0.0)
    return jnp.sum(spread, axis=0, keepdims=True)


def to_col(row):
    lane = lax.broadcasted_iota(jnp.int32, (8, 128), 1)
    sub = lax.broadcasted_iota(jnp.int32, (8, 128), 0)
    spread = jnp.where(lane == sub, jnp.broadcast_to(row, (8, 128)), 0.0)
    return jnp.sum(spread, axis=1, keepdims=True)


def wait_bytes(ref, sem):
    pltpu.make_async_copy(ref, ref, sem).wait()


def kernel(
    nsub, npatch, nslot, width,
    src, own, rank, keep, comp, slots, rhs_hbm, inv_hbm, out,
    inv, rhs, res, dirn, imag, sol, fsend, frecv, rsend, rrecv0, rrecv1, psend, precv,
    load, lhs, resp, slot_in, slot_sm, slot_vec, near, near_in, far, far_in, all_in,
    sems, psem_send, psem_recv, slot_send, slot_recv, rhs_sem, inv_sem, misc,
):
    rrecv = (rrecv0, rrecv1)
    b = lax.axis_index("body")
    me = lax.axis_index("sub")
    tile = (8, width)
    top = lax.broadcasted_iota(jnp.int32, tile, 0) < 4
    half = npatch // 2
    zero = jnp.zeros(tile, jnp.float32)

    def swap(v):
        return pltpu.roll(v, 4, 0)

    def peer(i):
        return lax.rem(me + i, nsub)

    def peers(body, unroll):
        def some(i, c):
            for u in range(unroll):
                body(peer(1 + i * unroll + u))
            return c

        whole = (nsub - 1) // unroll
        lax.fori_loop(0, whole, some, 0)
        for i in range(1 + whole * unroll, nsub):
            body(peer(i))

    def remote(src_ref, dst_ref, send, recv, p):
        return pltpu.make_async_remote_copy(
            src_ref=src_ref, dst_ref=dst_ref, send_sem=send, recv_sem=recv,
            device_id=(b, p), device_id_type=MESH,
        )

    rhs_copies = [
        pltpu.make_async_copy(rhs_hbm.at[c], rhs.at[:, c, :], rhs_sem.at[c]) for c in range(8)
    ]
    for copy in rhs_copies:
        copy.start()

    barrier = pltpu.get_barrier_semaphore()
    peers(
        lambda p: pl.semaphore_signal(barrier, inc=1, device_id=(b, p), device_id_type=MESH),
        ISSUE,
    )
    pl.semaphore_signal(barrier, inc=1, device_id=(1 - b, me), device_id_type=MESH)

    inv_copy = pltpu.make_async_copy(inv_hbm, inv, inv_sem)
    inv_copy.start()
    for copy in rhs_copies:
        copy.wait()

    def start_residual(i, accs):
        accs = list(accs)
        rows = comp[pl.ds(pl.multiple_of(i * UNROLL, UNROLL), UNROLL), :]
        for u in range(UNROLL):
            p = i * UNROLL + u
            v = keep[p] * rhs[p]
            w = swap(v)
            for g in range(GROUPS):
                t = jnp.where(top, v, w) if g == 0 else jnp.where(top, w, v)
                res[g, p] = t
                dirn[g, p] = zero
                imag[g, p] = zero
                sol[g, p] = zero
                square = t * t
                accs[g] = accs[g] + square
                accs[GROUPS + g] = accs[GROUPS + g] + rows[u:u + 1, :] * square
        return tuple(accs)

    accs = lax.fori_loop(0, npatch // UNROLL, start_residual, (zero,) * (2 * GROUPS))
    sums = [(accs[g], accs[GROUPS + g]) for g in range(GROUPS)]

    pl.semaphore_wait(barrier, nsub)

    def pack_forward(g, t):
        a = res[g, src[t * ROOM]]
        z = res[g, src[t * ROOM + 1]]
        fsend[g, t] = jnp.where(top, a, z)

    def forward(g):
        def one(p):
            pack_forward(g, p)
            remote(fsend.at[g, p], frecv.at[g, me], sems.at[FWD_SEND, g], sems.at[FWD_RECV, g], p).start()

        peers(one, ISSUE)
        pack_forward(g, me)
        pltpu.make_async_copy(fsend.at[g, me], frecv.at[g, me], sems.at[FWD_RECV, g]).start()

    def forward_sent(g):
        wait_bytes(fsend.at[g, pl.ds(0, nsub - 1)], sems.at[FWD_SEND, g])

    def return_sent(g):
        wait_bytes(rsend.at[g, pl.ds(0, nsub - 1)], sems.at[RET_SEND, g])

    def receive_forward(g):
        wait_bytes(frecv.at[g], sems.at[FWD_RECV, g])

        def gather(i, accs):
            accs = list(accs)
            for u in range(4):
                s = i * 4 + u
                v = frecv[g, s]
                which = slot_vec[s]
                for k in range(nslot):
                    accs[k] = accs[k] + jnp.where(which == k, v, 0.0)
            return tuple(accs)

        loads = lax.fori_loop(0, nsub // 4, gather, (zero,) * nslot)
        for k in range(nslot):
            v = loads[k] + swap(loads[k])
            load[k] = v
            high = v.astype(jnp.bfloat16).astype(jnp.float32)
            lhs[:, k * width:(k + 1) * width] = jnp.where(top, high, v - high).astype(jnp.bfloat16)

        def column(n, acc):
            cols = pl.ds(pl.multiple_of(n * width, width), width)
            o = jnp.dot(lhs[...], inv[:, cols], preferred_element_type=jnp.float32)
            o = o + swap(o)
            resp[n] = o
            return acc + load[n] * o

        return lax.fori_loop(0, nslot, column, zero)

    def pack_return(g, s):
        a = resp[jnp.maximum(slot_sm[s, 0, 0], 0)]
        z = resp[jnp.maximum(slot_sm[s, 0, 1], 0)]
        rsend[g, s] = jnp.where(top, a, z)

    def sums_row(loaded, squares):
        rr, rcr = squares
        image = loaded + jnp.where(b == 0, 1.0, 0.0) * rcr
        return to_row(jnp.sum(jnp.where(top, image, rr), axis=1, keepdims=True))

    block, place = me // SPAN, me % SPAN

    def send_near(g, row):
        near[g] = row
        for i in range(1, SPAN):
            p = block * SPAN + (place + i) % SPAN
            remote(near.at[g], near_in.at[g, place], sems.at[NEAR_SEND, g], sems.at[NEAR_RECV, g], p).start()
        pltpu.make_async_copy(near.at[g], near_in.at[g, place], sems.at[NEAR_RECV, g]).start()

    def send_far(g):
        wait_bytes(near_in.at[g], sems.at[NEAR_RECV, g])
        wait_bytes(near_in.at[g, pl.ds(0, SPAN - 1)], sems.at[NEAR_SEND, g])
        far[g] = jnp.sum(near_in[g], axis=0)
        for i in range(1, nsub // SPAN):
            p = (block + i) % (nsub // SPAN) * SPAN + place
            remote(far.at[g], far_in.at[g, block], sems.at[FAR_SEND, g], sems.at[FAR_RECV, g], p).start()
        pltpu.make_async_copy(far.at[g], far_in.at[g, block], sems.at[FAR_RECV, g]).start()

    def receive_far(g):
        wait_bytes(far_in.at[g], sems.at[FAR_RECV, g])
        wait_bytes(far_in.at[g, pl.ds(0, nsub // SPAN - 1)], sems.at[FAR_SEND, g])
        return jnp.sum(far_in[g], axis=0)

    def send_all(g, row):
        near[g] = row
        peers(
            lambda p: remote(near.at[g], all_in.at[g, me], sems.at[ALL_SEND, g], sems.at[ALL_RECV, g], p).start(),
            ISSUE,
        )
        pltpu.make_async_copy(near.at[g], all_in.at[g, me], sems.at[ALL_RECV, g]).start()

    def receive_all(g):
        wait_bytes(all_in.at[g], sems.at[ALL_RECV, g])
        wait_bytes(all_in.at[g, pl.ds(0, nsub - 1)], sems.at[ALL_SEND, g])
        return jnp.sum(all_in[g], axis=0)

    def send_back(g):
        def one(p):
            pack_return(g, p)
            remote(rsend.at[g, p], rrecv[g].at[me], sems.at[RET_SEND, g], sems.at[RET_RECV, g], p).start()

        peers(one, ISSUE)
        pack_return(g, me)
        pltpu.make_async_copy(rsend.at[g, me], rrecv[g].at[me], sems.at[RET_RECV, g]).start()

    def partner(g, par, part):
        first, size = ((0, 1 + half // 2), (1 + half // 2, half // 2), (0, 1))[part]
        return pltpu.make_async_remote_copy(
            src_ref=psend.at[g, pl.ds(first, size)], dst_ref=precv.at[par, g, pl.ds(first, size)],
            send_sem=psem_send.at[g, part % 2], recv_sem=psem_recv.at[par, g, part % 2],
            device_id=(1 - b, me), device_id_type=MESH,
        )

    def unfold(g, row):
        both = jnp.broadcast_to(to_col(row), tile)
        other = swap(both)
        image = jnp.where(top, both, other)
        psend[g, 0] = image
        return image, jnp.where(top, other, both)

    def steps(g, par, image, rr, rr_old, curve_old):
        beta = rr / rr_old
        return beta, image + precv[par, g, 0] - beta * beta * curve_old

    def receive_return(g, par, rr_old, curve_old):
        wait_bytes(rrecv[g], sems.at[RET_RECV, g])
        image, rr = unfold(g, receive_far(g))

        def pick(i, c):
            for u in range(4):
                p = i * 4 + u
                q = p + half
                a = rrecv[g][own[p]]
                z = rrecv[g][own[q]]
                a = jnp.where(rank[p] == 0, a, swap(a))
                z = jnp.where(rank[q] == 0, swap(z), z)
                psend[g, 1 + p] = jnp.where(top, a, z)
            return c

        lax.fori_loop(0, half // 8, pick, 0)
        first = partner(g, par, 0)
        first.start()
        lax.fori_loop(half // 8, half // 4, pick, 0)
        second = partner(g, par, 1)
        second.start()
        first.wait()
        beta, curve = steps(g, par, image, rr, rr_old, curve_old)
        alpha = rr / curve

        def update(i, accs):
            acc, acc2 = accs
            low = comp[pl.ds(pl.multiple_of(i * UNROLL, UNROLL), UNROLL), :]
            high = comp[pl.ds(pl.multiple_of(half + i * UNROLL, UNROLL), UNROLL), :]
            for u in range(UNROLL):
                p = i * UNROLL + u
                pair = psend[g, 1 + p] + precv[par, g, 1 + p]
                other = swap(pair)
                for rows, q, v in (
                    (low, p, jnp.where(top, pair, other)),
                    (high, p + half, jnp.where(top, other, pair)),
                ):
                    c = jnp.broadcast_to(rows[u:u + 1, :], tile)
                    r = res[g, q]
                    d = r + beta * dirn[g, q]
                    f = keep[q] * (v + c * r) + beta * imag[g, q]
                    dirn[g, q] = d
                    imag[g, q] = f
                    sol[g, q] = sol[g, q] + alpha * d
                    r = r - alpha * f
                    res[g, q] = r
                    square = r * r
                    acc = acc + square
                    acc2 = acc2 + c * square
            return acc, acc2

        squares = lax.fori_loop(0, half // UNROLL // 2, update, (zero, zero))
        second.wait()
        squares = lax.fori_loop(half // UNROLL // 2, half // UNROLL, update, squares)
        return squares, rr, curve

    forward(0)
    peers(lambda p: remote(slots.at[p], slot_in.at[me], slot_send, slot_recv, p).start(), ISSUE)
    pltpu.make_async_copy(slots.at[me], slot_in.at[me], slot_recv).start()
    forward_sent(0)
    forward(1)

    wait_bytes(slot_in, slot_recv)
    wait_bytes(slot_in.at[pl.ds(0, nsub - 1)], slot_send)
    slot_copy = pltpu.make_async_copy(slot_in, slot_sm, misc)
    slot_copy.start()
    inv_copy.wait()
    slot_copy.wait()

    def spread_slots(i, c):
        for u in range(4):
            s = i * 4 + u
            slot_vec[s] = jnp.where(top, slot_sm[s, 0, 0], slot_sm[s, 0, 1])
        return c

    lax.fori_loop(0, nsub // 4, spread_slots, 0)

    def iteration(k, carry):
        carry = list(carry)
        for g in range(GROUPS):
            row = sums_row(receive_forward(g), carry[g][0])
            if g > 0:
                send_far(g - 1)
            send_near(g, row)
            (forward_sent if g == 0 else return_sent)(1 - g)
            send_back(g)
        for g in range(GROUPS):
            carry[g] = receive_return(g, lax.rem(k, 2), *carry[g][1:])
            if g == 0:
                send_far(GROUPS - 1)
            (return_sent if g == 0 else forward_sent)(1 - g)
            forward(g)
        return tuple(carry)

    one = jnp.ones(tile, jnp.float32)
    carry = lax.fori_loop(0, ITERS - 1, iteration, tuple((sums[g], one, zero) for g in range(GROUPS)))
    par = (ITERS - 1) % 2
    for g in range(GROUPS):
        send_all(g, sums_row(receive_forward(g), carry[g][0]))
        if g == 0:
            forward_sent(1)
    last = []
    for g in range(GROUPS):
        image, rr = unfold(g, receive_all(g))
        copy = partner(g, par, 2)
        copy.start()
        copy.wait()
        beta, curve = steps(g, par, image, rr, carry[g][1], carry[g][2])
        last.append((rr / curve, beta))

    def finish(i, c):
        for u in range(UNROLL):
            p = i * UNROLL + u
            a, z = (
                sol[g, p] + last[g][0] * (res[g, p] + last[g][1] * dirn[g, p]) for g in range(GROUPS)
            )
            out[p] = jnp.where(top, a, z)
        return c

    lax.fori_loop(0, npatch // UNROLL, finish, 0)


def on_device(nsub, rhs, compliance, plate_owner, found_owner, slot_pairs, active, inverse):
    side = lax.axis_index("body")
    ncase, npatch, width = rhs.shape
    iface = inverse.shape[-1]
    nslot = iface // width
    nrow = nsub * ROOM
    owner = jnp.where(side == 0, plate_owner[:, 0], found_owner[:, 0])
    slot = jnp.where(side == 0, slot_pairs[:, 0], slot_pairs[:, 1])
    patch = jnp.arange(npatch, dtype=jnp.int32)
    same = (patch[None, :] < patch[:, None]) & (owner[None, :] == owner[:, None])
    rank = jnp.sum(same.astype(jnp.int32), axis=1)
    placed = (owner * ROOM + rank)[None, :] == jnp.arange(nrow, dtype=jnp.int32)[:, None]
    source = jnp.sum(jnp.where(placed, patch[None, :], 0), axis=1)
    sent_slot = jnp.sum(jnp.where(placed, slot[None, :] + 1, 0), axis=1) - 1
    slots = jnp.pad(sent_slot.reshape(nsub, 1, ROOM), ((0, 0), (0, 0), (0, 128 - ROOM)))
    keep = active.astype(jnp.float32)

    f32, i32 = jnp.float32, jnp.int32
    vmem = pl.BlockSpec(memory_space=pltpu.VMEM)
    smem = pl.BlockSpec(memory_space=pltpu.SMEM)
    hbm = pl.BlockSpec(memory_space=pl.ANY)
    state = pltpu.VMEM((GROUPS, npatch, 8, width), f32)
    message = pltpu.VMEM((GROUPS, nsub, 8, width), f32)
    single = pltpu.VMEM((nsub, 8, width), f32)
    half = npatch // 2
    result = pl.pallas_call(
        functools.partial(kernel, nsub, npatch, nslot, width),
        out_shape=jax.ShapeDtypeStruct((npatch, ncase, width), f32),
        in_specs=[smem, smem, smem, smem, vmem, vmem, hbm, hbm],
        out_specs=vmem,
        scratch_shapes=[
            pltpu.VMEM((iface, iface), jnp.bfloat16),
            single, state, state, state, state, message, message, message, single, single,
            pltpu.VMEM((GROUPS, half + 1, 8, width), f32),
            pltpu.VMEM((2, GROUPS, half + 1, 8, width), f32),
            pltpu.VMEM((nslot, 8, width), f32),
            pltpu.VMEM((8, iface), jnp.bfloat16),
            pltpu.VMEM((nslot, 8, width), f32),
            pltpu.VMEM((nsub, 1, 128), i32),
            pltpu.SMEM((nsub, 1, 128), i32),
            pltpu.VMEM((nsub, 8, width), i32),
            pltpu.VMEM((GROUPS, 1, 128), f32),
            pltpu.VMEM((GROUPS, SPAN, 1, 128), f32),
            pltpu.VMEM((GROUPS, 1, 128), f32),
            pltpu.VMEM((GROUPS, nsub // SPAN, 1, 128), f32),
            pltpu.VMEM((GROUPS, nsub, 1, 128), f32),
            pltpu.SemaphoreType.DMA((10, GROUPS)),
            pltpu.SemaphoreType.DMA((GROUPS, 2)),
            pltpu.SemaphoreType.DMA((2, GROUPS, 2)),
            pltpu.SemaphoreType.DMA,
            pltpu.SemaphoreType.DMA,
            pltpu.SemaphoreType.DMA((8,)),
            pltpu.SemaphoreType.DMA,
            pltpu.SemaphoreType.DMA,
        ],
        compiler_params=pltpu.CompilerParams(
            collective_id=0, has_side_effects=True, vmem_limit_bytes=48 * 2**20
        ),
    )(source, owner, rank, keep, compliance, slots, rhs, inverse[0, 0])
    return jnp.transpose(result, (1, 0, 2))


def solution(mesh):
    in_specs = (
        P(None, "sub", None),
        P("sub", None),
        P("sub", None),
        P("sub", None),
        P("sub", None),
        P("sub"),
        P("body", "sub", None, None),
    )
    return jax.shard_map(
        functools.partial(on_device, mesh.shape["sub"]),
        mesh=mesh, in_specs=in_specs, out_specs=P(None, "sub", None), check_vma=False,
    )
```

```python
import functools
import jax
import jax.numpy as jnp
from jax import lax
from jax.experimental import pallas as pl
from jax.experimental.pallas import tpu as pltpu
from jax.sharding import PartitionSpec as P

ITERS = 4
GROUPS = 2
ROOM = 2
UNROLL = 8
ISSUE = 3
SPAN = 8
CUT = 60
MESH = pl.DeviceIdType.MESH
FWD_SEND, FWD_RECV, RET_SEND, RET_RECV = range(4)
NEAR_SEND, NEAR_RECV, FAR_SEND, FAR_RECV, ALL_SEND, ALL_RECV = range(4, 10)


def to_row(col):
    lane = lax.broadcasted_iota(jnp.int32, (8, 128), 1)
    sub = lax.broadcasted_iota(jnp.int32, (8, 128), 0)
    spread = jnp.where(lane == sub, jnp.broadcast_to(col, (8, 128)), 0.0)
    return jnp.sum(spread, axis=0, keepdims=True)


def to_col(row):
    lane = lax.broadcasted_iota(jnp.int32, (8, 128), 1)
    sub = lax.broadcasted_iota(jnp.int32, (8, 128), 0)
    spread = jnp.where(lane == sub, jnp.broadcast_to(row, (8, 128)), 0.0)
    return jnp.sum(spread, axis=1, keepdims=True)


def wait_bytes(ref, sem):
    pltpu.make_async_copy(ref, ref, sem).wait()


def kernel(
    nsub, npatch, nslot, width,
    src, own, rank, keep, comp, slots, rhs_hbm, inv_hbm, out,
    inv, rhs, res, dirn, imag, sol, fsend, frecv, rsend, rrecv0, rrecv1, psend, precv,
    load, lhs, resp, slot_in, slot_sm, slot_vec, near, near_in, far, far_in, all_in,
    sems, psem_send, psem_recv, slot_send, slot_recv, rhs_sem, inv_sem, misc,
):
    rrecv = (rrecv0, rrecv1)
    b = lax.axis_index("body")
    me = lax.axis_index("sub")
    tile = (8, width)
    top = lax.broadcasted_iota(jnp.int32, tile, 0) < 4
    half = npatch // 2
    zero = jnp.zeros(tile, jnp.float32)

    def swap(v):
        return pltpu.roll(v, 4, 0)

    def peer(i):
        return lax.rem(me + i, nsub)

    def peers(body, unroll, first=1, stop=None):
        stop = nsub if stop is None else stop

        def some(i, c):
            for u in range(unroll):
                body(peer(first + i * unroll + u))
            return c

        whole = (stop - first) // unroll
        lax.fori_loop(0, whole, some, 0)
        for i in range(first + whole * unroll, stop):
            body(peer(i))

    def remote(src_ref, dst_ref, send, recv, p):
        return pltpu.make_async_remote_copy(
            src_ref=src_ref, dst_ref=dst_ref, send_sem=send, recv_sem=recv,
            device_id=(b, p), device_id_type=MESH,
        )

    rhs_copies = [
        pltpu.make_async_copy(rhs_hbm.at[c], rhs.at[:, c, :], rhs_sem.at[c]) for c in range(8)
    ]
    for copy in rhs_copies:
        copy.start()

    barrier = pltpu.get_barrier_semaphore()
    peers(
        lambda p: pl.semaphore_signal(barrier, inc=1, device_id=(b, p), device_id_type=MESH),
        ISSUE,
    )
    pl.semaphore_signal(barrier, inc=1, device_id=(1 - b, me), device_id_type=MESH)

    inv_copy = pltpu.make_async_copy(inv_hbm, inv, inv_sem)
    inv_copy.start()
    for copy in rhs_copies:
        copy.wait()

    def start_residual(i, accs):
        accs = list(accs)
        rows = comp[pl.ds(pl.multiple_of(i * UNROLL, UNROLL), UNROLL), :]
        for u in range(UNROLL):
            p = i * UNROLL + u
            v = keep[p] * rhs[p]
            w = swap(v)
            for g in range(GROUPS):
                t = jnp.where(top, v, w) if g == 0 else jnp.where(top, w, v)
                res[g, p] = t
                dirn[g, p] = zero
                imag[g, p] = zero
                sol[g, p] = zero
                square = t * t
                accs[g] = accs[g] + square
                accs[GROUPS + g] = accs[GROUPS + g] + rows[u:u + 1, :] * square
        return tuple(accs)

    accs = lax.fori_loop(0, npatch // UNROLL, start_residual, (zero,) * (2 * GROUPS))
    sums = [(accs[g], accs[GROUPS + g]) for g in range(GROUPS)]

    pl.semaphore_wait(barrier, nsub)

    def pack_forward(g, t):
        a = res[g, src[t * ROOM]]
        z = res[g, src[t * ROOM + 1]]
        fsend[g, t] = jnp.where(top, a, z)

    def forward(g, first=1, stop=nsub):
        def one(p):
            pack_forward(g, p)
            remote(fsend.at[g, p], frecv.at[g, me], sems.at[FWD_SEND, g], sems.at[FWD_RECV, g], p).start()

        peers(one, ISSUE, first, stop)
        if stop < nsub:
            return
        pack_forward(g, me)
        pltpu.make_async_copy(fsend.at[g, me], frecv.at[g, me], sems.at[FWD_RECV, g]).start()

    def forward_sent(g):
        wait_bytes(fsend.at[g, pl.ds(0, nsub - 1)], sems.at[FWD_SEND, g])

    def return_sent(g):
        wait_bytes(rsend.at[g, pl.ds(0, nsub - 1)], sems.at[RET_SEND, g])

    def receive_forward(g):
        wait_bytes(frecv.at[g], sems.at[FWD_RECV, g])

        def gather(i, accs):
            accs = list(accs)
            for u in range(4):
                s = i * 4 + u
                v = frecv[g, s]
                which = slot_vec[s]
                for k in range(nslot):
                    accs[k] = accs[k] + jnp.where(which == k, v, 0.0)
            return tuple(accs)

        loads = lax.fori_loop(0, nsub // 4, gather, (zero,) * nslot)
        for k in range(nslot):
            v = loads[k] + swap(loads[k])
            load[k] = v
            high = v.astype(jnp.bfloat16).astype(jnp.float32)
            lhs[:, k * width:(k + 1) * width] = jnp.where(top, high, v - high).astype(jnp.bfloat16)

        acc = zero
        for n in range(nslot):
            o = jnp.dot(
                lhs[...], inv[:, n * width:(n + 1) * width], preferred_element_type=jnp.float32
            )
            o = o + swap(o)
            resp[n] = o
            acc = acc + load[n] * o
        return acc

    def pack_return(g, s):
        a = resp[jnp.maximum(slot_sm[s, 0, 0], 0)]
        z = resp[jnp.maximum(slot_sm[s, 0, 1], 0)]
        rsend[g, s] = jnp.where(top, a, z)

    def sums_row(loaded, squares):
        rr, rcr = squares
        image = loaded + jnp.where(b == 0, 1.0, 0.0) * rcr
        return to_row(jnp.sum(jnp.where(top, image, rr), axis=1, keepdims=True))

    block, place = me // SPAN, me % SPAN

    def send_near(g, row):
        near[g] = row
        for i in range(1, SPAN):
            p = block * SPAN + (place + i) % SPAN
            remote(near.at[g], near_in.at[g, place], sems.at[NEAR_SEND, g], sems.at[NEAR_RECV, g], p).start()
        pltpu.make_async_copy(near.at[g], near_in.at[g, place], sems.at[NEAR_RECV, g]).start()

    def send_far(g):
        wait_bytes(near_in.at[g], sems.at[NEAR_RECV, g])
        wait_bytes(near_in.at[g, pl.ds(0, SPAN - 1)], sems.at[NEAR_SEND, g])
        far[g] = jnp.sum(near_in[g], axis=0)
        for i in range(1, nsub // SPAN):
            p = (block + i) % (nsub // SPAN) * SPAN + place
            remote(far.at[g], far_in.at[g, block], sems.at[FAR_SEND, g], sems.at[FAR_RECV, g], p).start()
        pltpu.make_async_copy(far.at[g], far_in.at[g, block], sems.at[FAR_RECV, g]).start()

    def receive_far(g):
        wait_bytes(far_in.at[g], sems.at[FAR_RECV, g])
        wait_bytes(far_in.at[g, pl.ds(0, nsub // SPAN - 1)], sems.at[FAR_SEND, g])
        return jnp.sum(far_in[g], axis=0)

    def send_all(g, row):
        near[g] = row
        peers(
            lambda p: remote(near.at[g], all_in.at[g, me], sems.at[ALL_SEND, g], sems.at[ALL_RECV, g], p).start(),
            ISSUE,
        )
        pltpu.make_async_copy(near.at[g], all_in.at[g, me], sems.at[ALL_RECV, g]).start()

    def receive_all(g):
        wait_bytes(all_in.at[g], sems.at[ALL_RECV, g])
        wait_bytes(all_in.at[g, pl.ds(0, nsub - 1)], sems.at[ALL_SEND, g])
        return jnp.sum(all_in[g], axis=0)

    def send_back(g, first=1, stop=nsub):
        def one(p):
            pack_return(g, p)
            remote(rsend.at[g, p], rrecv[g].at[me], sems.at[RET_SEND, g], sems.at[RET_RECV, g], p).start()

        peers(one, ISSUE, first, stop)
        if stop < nsub:
            return
        pack_return(g, me)
        pltpu.make_async_copy(rsend.at[g, me], rrecv[g].at[me], sems.at[RET_RECV, g]).start()

    def partner(g, par, part):
        first, size = ((0, 1 + half // 2), (1 + half // 2, half // 2), (0, 1))[part]
        return pltpu.make_async_remote_copy(
            src_ref=psend.at[g, pl.ds(first, size)], dst_ref=precv.at[par, g, pl.ds(first, size)],
            send_sem=psem_send.at[g, part % 2], recv_sem=psem_recv.at[par, g, part % 2],
            device_id=(1 - b, me), device_id_type=MESH,
        )

    def unfold(g, row):
        both = jnp.broadcast_to(to_col(row), tile)
        other = swap(both)
        image = jnp.where(top, both, other)
        psend[g, 0] = image
        return image, jnp.where(top, other, both)

    def steps(g, par, image, rr, rr_old, curve_old):
        beta = rr / rr_old
        return beta, image + precv[par, g, 0] - beta * beta * curve_old

    def receive_return(g, par, rr_old, curve_old, meanwhile):
        wait_bytes(rrecv[g], sems.at[RET_RECV, g])
        image, rr = unfold(g, receive_far(g))

        def pick(i, c):
            for u in range(4):
                p = i * 4 + u
                q = p + half
                a = rrecv[g][own[p]]
                z = rrecv[g][own[q]]
                a = jnp.where(rank[p] == 0, a, swap(a))
                z = jnp.where(rank[q] == 0, swap(z), z)
                psend[g, 1 + p] = jnp.where(top, a, z)
            return c

        lax.fori_loop(0, half // 8, pick, 0)
        first = partner(g, par, 0)
        first.start()
        lax.fori_loop(half // 8, half // 4, pick, 0)
        second = partner(g, par, 1)
        second.start()
        meanwhile()
        first.wait()
        beta, curve = steps(g, par, image, rr, rr_old, curve_old)
        alpha = rr / curve

        def update(i, accs):
            acc, acc2 = accs
            low = comp[pl.ds(pl.multiple_of(i * UNROLL, UNROLL), UNROLL), :]
            high = comp[pl.ds(pl.multiple_of(half + i * UNROLL, UNROLL), UNROLL), :]
            for u in range(UNROLL):
                p = i * UNROLL + u
                pair = psend[g, 1 + p] + precv[par, g, 1 + p]
                other = swap(pair)
                for rows, q, v in (
                    (low, p, jnp.where(top, pair, other)),
                    (high, p + half, jnp.where(top, other, pair)),
                ):
                    c = jnp.broadcast_to(rows[u:u + 1, :], tile)
                    r = res[g, q]
                    d = r + beta * dirn[g, q]
                    f = keep[q] * (v + c * r) + beta * imag[g, q]
                    dirn[g, q] = d
                    imag[g, q] = f
                    sol[g, q] = sol[g, q] + alpha * d
                    r = r - alpha * f
                    res[g, q] = r
                    square = r * r
                    acc = acc + square
                    acc2 = acc2 + c * square
            return acc, acc2

        squares = lax.fori_loop(0, half // UNROLL // 2, update, (zero, zero))
        second.wait()
        squares = lax.fori_loop(half // UNROLL // 2, half // UNROLL, update, squares)
        return squares, rr, curve

    forward(0)
    peers(lambda p: remote(slots.at[p], slot_in.at[me], slot_send, slot_recv, p).start(), ISSUE)
    pltpu.make_async_copy(slots.at[me], slot_in.at[me], slot_recv).start()
    forward_sent(0)
    forward(1)

    wait_bytes(slot_in, slot_recv)
    wait_bytes(slot_in.at[pl.ds(0, nsub - 1)], slot_send)
    slot_copy = pltpu.make_async_copy(slot_in, slot_sm, misc)
    slot_copy.start()
    inv_copy.wait()
    slot_copy.wait()

    def spread_slots(i, c):
        for u in range(4):
            s = i * 4 + u
            slot_vec[s] = jnp.where(top, slot_sm[s, 0, 0], slot_sm[s, 0, 1])
        return c

    lax.fori_loop(0, nsub // 4, spread_slots, 0)

    def iteration(k, carry):
        carry = list(carry)
        for g in range(GROUPS):
            row = sums_row(receive_forward(g), carry[g][0])
            if g > 0:
                send_far(g - 1)
            send_near(g, row)
            (forward_sent if g == 0 else return_sent)(1 - g)
            send_back(g, 1, nsub if g == 0 else CUT)

        def rest_of_return():
            send_back(1, CUT)
            send_far(1)

        carry[0] = receive_return(0, lax.rem(k, 2), *carry[0][1:], rest_of_return)
        return_sent(1)
        forward(0, 1, CUT)
        carry[1] = receive_return(1, lax.rem(k, 2), *carry[1][1:], lambda: forward(0, CUT))
        forward_sent(0)
        forward(1)
        return tuple(carry)

    one = jnp.ones(tile, jnp.float32)
    carry = lax.fori_loop(0, ITERS - 1, iteration, tuple((sums[g], one, zero) for g in range(GROUPS)))
    par = (ITERS - 1) % 2
    for g in range(GROUPS):
        send_all(g, sums_row(receive_forward(g), carry[g][0]))
        if g == 0:
            forward_sent(1)
    ends = []
    for g in range(GROUPS):
        ends.append(unfold(g, receive_all(g)))
        partner(g, par, 2).start()
    last = []
    for g in range(GROUPS):
        partner(g, par, 2).wait()
        beta, curve = steps(g, par, *ends[g], carry[g][1], carry[g][2])
        last.append((ends[g][1] / curve, beta))

    def finish(i, c):
        for u in range(UNROLL):
            p = i * UNROLL + u
            a, z = (
                sol[g, p] + last[g][0] * (res[g, p] + last[g][1] * dirn[g, p]) for g in range(GROUPS)
            )
            out[p] = jnp.where(top, a, z)
        return c

    lax.fori_loop(0, npatch // UNROLL, finish, 0)


def on_device(nsub, rhs, compliance, plate_owner, found_owner, slot_pairs, active, inverse):
    side = lax.axis_index("body")
    ncase, npatch, width = rhs.shape
    iface = inverse.shape[-1]
    nslot = iface // width
    nrow = nsub * ROOM
    owner = jnp.where(side == 0, plate_owner[:, 0], found_owner[:, 0])
    slot = jnp.where(side == 0, slot_pairs[:, 0], slot_pairs[:, 1])
    patch = jnp.arange(npatch, dtype=jnp.int32)
    same = (patch[None, :] < patch[:, None]) & (owner[None, :] == owner[:, None])
    rank = jnp.sum(same.astype(jnp.int32), axis=1)
    placed = (owner * ROOM + rank)[None, :] == jnp.arange(nrow, dtype=jnp.int32)[:, None]
    source = jnp.sum(jnp.where(placed, patch[None, :], 0), axis=1)
    sent_slot = jnp.sum(jnp.where(placed, slot[None, :] + 1, 0), axis=1) - 1
    slots = jnp.pad(sent_slot.reshape(nsub, 1, ROOM), ((0, 0), (0, 0), (0, 128 - ROOM)))
    keep = active.astype(jnp.float32)

    f32, i32 = jnp.float32, jnp.int32
    vmem = pl.BlockSpec(memory_space=pltpu.VMEM)
    smem = pl.BlockSpec(memory_space=pltpu.SMEM)
    hbm = pl.BlockSpec(memory_space=pl.ANY)
    state = pltpu.VMEM((GROUPS, npatch, 8, width), f32)
    message = pltpu.VMEM((GROUPS, nsub, 8, width), f32)
    single = pltpu.VMEM((nsub, 8, width), f32)
    half = npatch // 2
    result = pl.pallas_call(
        functools.partial(kernel, nsub, npatch, nslot, width),
        out_shape=jax.ShapeDtypeStruct((npatch, ncase, width), f32),
        in_specs=[smem, smem, smem, smem, vmem, vmem, hbm, hbm],
        out_specs=vmem,
        scratch_shapes=[
            pltpu.VMEM((iface, iface), jnp.bfloat16),
            single, state, state, state, state, message, message, message, single, single,
            pltpu.VMEM((GROUPS, half + 1, 8, width), f32),
            pltpu.VMEM((2, GROUPS, half + 1, 8, width), f32),
            pltpu.VMEM((nslot, 8, width), f32),
            pltpu.VMEM((8, iface), jnp.bfloat16),
            pltpu.VMEM((nslot, 8, width), f32),
            pltpu.VMEM((nsub, 1, 128), i32),
            pltpu.SMEM((nsub, 1, 128), i32),
            pltpu.VMEM((nsub, 8, width), i32),
            pltpu.VMEM((GROUPS, 1, 128), f32),
            pltpu.VMEM((GROUPS, SPAN, 1, 128), f32),
            pltpu.VMEM((GROUPS, 1, 128), f32),
            pltpu.VMEM((GROUPS, nsub // SPAN, 1, 128), f32),
            pltpu.VMEM((GROUPS, nsub, 1, 128), f32),
            pltpu.SemaphoreType.DMA((10, GROUPS)),
            pltpu.SemaphoreType.DMA((GROUPS, 2)),
            pltpu.SemaphoreType.DMA((2, GROUPS, 2)),
            pltpu.SemaphoreType.DMA,
            pltpu.SemaphoreType.DMA,
            pltpu.SemaphoreType.DMA((8,)),
            pltpu.SemaphoreType.DMA,
            pltpu.SemaphoreType.DMA,
        ],
        compiler_params=pltpu.CompilerParams(
            collective_id=0, has_side_effects=True, vmem_limit_bytes=48 * 2**20
        ),
    )(source, owner, rank, keep, compliance, slots, rhs, inverse[0, 0])
    return jnp.transpose(result, (1, 0, 2))


def solution(mesh):
    in_specs = (
        P(None, "sub", None),
        P("sub", None),
        P("sub", None),
        P("sub", None),
        P("sub", None),
        P("sub"),
        P("body", "sub", None, None),
    )
    return jax.shard_map(
        functools.partial(on_device, mesh.shape["sub"]),
        mesh=mesh, in_specs=in_specs, out_specs=P(None, "sub", None), check_vma=False,
    )
```

```python
import functools
import jax
import jax.numpy as jnp
from jax import lax
from jax.experimental import pallas as pl
from jax.experimental.pallas import tpu as pltpu
from jax.sharding import PartitionSpec as P

ITERS = 4
GROUPS = 2
ROOM = 2
UNROLL = 8
ISSUE = 3
SPAN = 8
CUT = 60
MESH = pl.DeviceIdType.MESH
FWD_SEND, FWD_RECV, RET_SEND, RET_RECV = range(4)
NEAR_SEND, NEAR_RECV, FAR_SEND, FAR_RECV, ALL_SEND, ALL_RECV = range(4, 10)


def to_row(col):
    lane = lax.broadcasted_iota(jnp.int32, (8, 128), 1)
    sub = lax.broadcasted_iota(jnp.int32, (8, 128), 0)
    spread = jnp.where(lane == sub, jnp.broadcast_to(col, (8, 128)), 0.0)
    return jnp.sum(spread, axis=0, keepdims=True)


def to_col(row):
    lane = lax.broadcasted_iota(jnp.int32, (8, 128), 1)
    sub = lax.broadcasted_iota(jnp.int32, (8, 128), 0)
    spread = jnp.where(lane == sub, jnp.broadcast_to(row, (8, 128)), 0.0)
    return jnp.sum(spread, axis=1, keepdims=True)


def wait_bytes(ref, sem):
    pltpu.make_async_copy(ref, ref, sem).wait()


def kernel(
    nsub, npatch, nslot, width,
    src, own, rank, keep, comp, slots, rhs_hbm, inv_hbm, out,
    inv, rhs, res, dirn, imag, sol, fsend, frecv, rsend, rrecv0, rrecv1, psend, precv,
    load, lhs, resp, slot_in, slot_sm, slot_vec, near, near_in, far, far_in, all_in,
    sems, psem_send, psem_recv, slot_send, slot_recv, rhs_sem, inv_sem, misc,
):
    rrecv = (rrecv0, rrecv1)
    b = lax.axis_index("body")
    me = lax.axis_index("sub")
    tile = (8, width)
    top = lax.broadcasted_iota(jnp.int32, tile, 0) < 4
    half = npatch // 2
    zero = jnp.zeros(tile, jnp.float32)

    def swap(v):
        return pltpu.roll(v, 4, 0)

    def peer(i):
        return lax.rem(me + i, nsub)

    def peers(body, unroll, first=1, stop=None):
        stop = nsub if stop is None else stop

        def some(i, c):
            for u in range(unroll):
                body(peer(first + i * unroll + u))
            return c

        whole = (stop - first) // unroll
        lax.fori_loop(0, whole, some, 0)
        for i in range(first + whole * unroll, stop):
            body(peer(i))

    def remote(src_ref, dst_ref, send, recv, p):
        return pltpu.make_async_remote_copy(
            src_ref=src_ref, dst_ref=dst_ref, send_sem=send, recv_sem=recv,
            device_id=(b, p), device_id_type=MESH,
        )

    rhs_copies = [
        pltpu.make_async_copy(rhs_hbm.at[c], rhs.at[:, c, :], rhs_sem.at[c]) for c in range(8)
    ]
    for copy in rhs_copies:
        copy.start()

    barrier = pltpu.get_barrier_semaphore()
    peers(
        lambda p: pl.semaphore_signal(barrier, inc=1, device_id=(b, p), device_id_type=MESH),
        ISSUE,
    )
    pl.semaphore_signal(barrier, inc=1, device_id=(1 - b, me), device_id_type=MESH)

    inv_copy = pltpu.make_async_copy(inv_hbm, inv, inv_sem)
    inv_copy.start()
    for copy in rhs_copies:
        copy.wait()

    def start_residual(i, accs):
        accs = list(accs)
        rows = comp[pl.ds(pl.multiple_of(i * UNROLL, UNROLL), UNROLL), :]
        for u in range(UNROLL):
            p = i * UNROLL + u
            v = keep[p].astype(jnp.float32) * rhs[p]
            w = swap(v)
            for g in range(GROUPS):
                t = jnp.where(top, v, w) if g == 0 else jnp.where(top, w, v)
                res[g, p] = t
                dirn[g, p] = zero
                imag[g, p] = zero
                sol[g, p] = zero
                square = t * t
                accs[g] = accs[g] + square
                accs[GROUPS + g] = accs[GROUPS + g] + rows[u:u + 1, :] * square
        return tuple(accs)

    accs = lax.fori_loop(0, npatch // UNROLL, start_residual, (zero,) * (2 * GROUPS))
    sums = [(accs[g], accs[GROUPS + g]) for g in range(GROUPS)]

    pl.semaphore_wait(barrier, nsub)

    def pack_forward(g, t):
        a = res[g, src[t * ROOM]]
        z = res[g, src[t * ROOM + 1]]
        fsend[g, t] = jnp.where(top, a, z)

    def forward(g, first=1, stop=nsub):
        def one(p):
            pack_forward(g, p)
            remote(fsend.at[g, p], frecv.at[g, me], sems.at[FWD_SEND, g], sems.at[FWD_RECV, g], p).start()

        peers(one, ISSUE, first, stop)
        if stop < nsub:
            return
        pack_forward(g, me)
        pltpu.make_async_copy(fsend.at[g, me], frecv.at[g, me], sems.at[FWD_RECV, g]).start()

    def forward_sent(g):
        wait_bytes(fsend.at[g, pl.ds(0, nsub - 1)], sems.at[FWD_SEND, g])

    def return_sent(g):
        wait_bytes(rsend.at[g, pl.ds(0, nsub - 1)], sems.at[RET_SEND, g])

    def receive_forward(g):
        wait_bytes(frecv.at[g], sems.at[FWD_RECV, g])

        def gather(i, accs):
            accs = list(accs)
            for u in range(4):
                s = i * 4 + u
                v = frecv[g, s]
                which = slot_vec[s]
                for k in range(nslot):
                    accs[k] = accs[k] + jnp.where(which == k, v, 0.0)
            return tuple(accs)

        loads = lax.fori_loop(0, nsub // 4, gather, (zero,) * nslot)
        for k in range(nslot):
            v = loads[k] + swap(loads[k])
            load[k] = v
            high = v.astype(jnp.bfloat16).astype(jnp.float32)
            lhs[:, k * width:(k + 1) * width] = jnp.where(top, high, v - high).astype(jnp.bfloat16)

        acc = zero
        for n in range(nslot):
            o = jnp.dot(
                lhs[...], inv[:, n * width:(n + 1) * width], preferred_element_type=jnp.float32
            )
            o = o + swap(o)
            resp[n] = o
            acc = acc + load[n] * o
        return acc

    def pack_return(g, s):
        a = resp[jnp.maximum(slot_sm[s, 0, 0], 0)]
        z = resp[jnp.maximum(slot_sm[s, 0, 1], 0)]
        rsend[g, s] = jnp.where(top, a, z)

    def sums_row(loaded, squares):
        rr, rcr = squares
        image = loaded + jnp.where(b == 0, 1.0, 0.0) * rcr
        return to_row(jnp.sum(jnp.where(top, image, rr), axis=1, keepdims=True))

    block, place = me // SPAN, me % SPAN

    def send_near(g, row):
        near[g] = row
        for i in range(1, SPAN):
            p = block * SPAN + (place + i) % SPAN
            remote(near.at[g], near_in.at[g, place], sems.at[NEAR_SEND, g], sems.at[NEAR_RECV, g], p).start()
        pltpu.make_async_copy(near.at[g], near_in.at[g, place], sems.at[NEAR_RECV, g]).start()

    def send_far(g):
        wait_bytes(near_in.at[g], sems.at[NEAR_RECV, g])
        wait_bytes(near_in.at[g, pl.ds(0, SPAN - 1)], sems.at[NEAR_SEND, g])
        far[g] = jnp.sum(near_in[g], axis=0)
        for i in range(1, nsub // SPAN):
            p = (block + i) % (nsub // SPAN) * SPAN + place
            remote(far.at[g], far_in.at[g, block], sems.at[FAR_SEND, g], sems.at[FAR_RECV, g], p).start()
        pltpu.make_async_copy(far.at[g], far_in.at[g, block], sems.at[FAR_RECV, g]).start()

    def receive_far(g):
        wait_bytes(far_in.at[g], sems.at[FAR_RECV, g])
        wait_bytes(far_in.at[g, pl.ds(0, nsub // SPAN - 1)], sems.at[FAR_SEND, g])
        return jnp.sum(far_in[g], axis=0)

    def send_all(g, row):
        near[g] = row
        peers(
            lambda p: remote(near.at[g], all_in.at[g, me], sems.at[ALL_SEND, g], sems.at[ALL_RECV, g], p).start(),
            ISSUE,
        )
        pltpu.make_async_copy(near.at[g], all_in.at[g, me], sems.at[ALL_RECV, g]).start()

    def receive_all(g):
        wait_bytes(all_in.at[g], sems.at[ALL_RECV, g])
        wait_bytes(all_in.at[g, pl.ds(0, nsub - 1)], sems.at[ALL_SEND, g])
        return jnp.sum(all_in[g], axis=0)

    def send_back(g, first=1, stop=nsub):
        def one(p):
            pack_return(g, p)
            remote(rsend.at[g, p], rrecv[g].at[me], sems.at[RET_SEND, g], sems.at[RET_RECV, g], p).start()

        peers(one, ISSUE, first, stop)
        if stop < nsub:
            return
        pack_return(g, me)
        pltpu.make_async_copy(rsend.at[g, me], rrecv[g].at[me], sems.at[RET_RECV, g]).start()

    def partner(g, par, part):
        first, size = ((0, 1 + half // 2), (1 + half // 2, half // 2), (0, 1))[part]
        return pltpu.make_async_remote_copy(
            src_ref=psend.at[g, pl.ds(first, size)], dst_ref=precv.at[par, g, pl.ds(first, size)],
            send_sem=psem_send.at[g, part % 2], recv_sem=psem_recv.at[par, g, part % 2],
            device_id=(1 - b, me), device_id_type=MESH,
        )

    def unfold(g, row):
        both = jnp.broadcast_to(to_col(row), tile)
        other = swap(both)
        image = jnp.where(top, both, other)
        psend[g, 0] = image
        return image, jnp.where(top, other, both)

    def steps(g, par, image, rr, rr_old, curve_old):
        beta = rr / rr_old
        return beta, image + precv[par, g, 0] - beta * beta * curve_old

    def receive_return(g, par, rr_old, curve_old, meanwhile):
        wait_bytes(rrecv[g], sems.at[RET_RECV, g])
        image, rr = unfold(g, receive_far(g))

        def pick(i, c):
            for u in range(4):
                p = i * 4 + u
                q = p + half
                a = rrecv[g][own[p]]
                z = rrecv[g][own[q]]
                a = jnp.where(rank[p] == 0, a, swap(a))
                z = jnp.where(rank[q] == 0, swap(z), z)
                psend[g, 1 + p] = jnp.where(top, a, z)
            return c

        lax.fori_loop(0, half // 8, pick, 0)
        first = partner(g, par, 0)
        first.start()
        lax.fori_loop(half // 8, half // 4, pick, 0)
        second = partner(g, par, 1)
        second.start()
        meanwhile()
        first.wait()
        beta, curve = steps(g, par, image, rr, rr_old, curve_old)
        alpha = rr / curve

        def update(i, accs):
            acc, acc2 = accs
            low = comp[pl.ds(pl.multiple_of(i * UNROLL, UNROLL), UNROLL), :]
            high = comp[pl.ds(pl.multiple_of(half + i * UNROLL, UNROLL), UNROLL), :]
            for u in range(UNROLL):
                p = i * UNROLL + u
                pair = psend[g, 1 + p] + precv[par, g, 1 + p]
                other = swap(pair)
                for rows, q, v in (
                    (low, p, jnp.where(top, pair, other)),
                    (high, p + half, jnp.where(top, other, pair)),
                ):
                    c = jnp.broadcast_to(rows[u:u + 1, :], tile)
                    r = res[g, q]
                    d = r + beta * dirn[g, q]
                    f = keep[q].astype(jnp.float32) * (v + c * r) + beta * imag[g, q]
                    dirn[g, q] = d
                    imag[g, q] = f
                    sol[g, q] = sol[g, q] + alpha * d
                    r = r - alpha * f
                    res[g, q] = r
                    square = r * r
                    acc = acc + square
                    acc2 = acc2 + c * square
            return acc, acc2

        squares = lax.fori_loop(0, half // UNROLL // 2, update, (zero, zero))
        second.wait()
        squares = lax.fori_loop(half // UNROLL // 2, half // UNROLL, update, squares)
        return squares, rr, curve

    forward(0)
    peers(lambda p: remote(slots.at[p], slot_in.at[me], slot_send, slot_recv, p).start(), ISSUE)
    pltpu.make_async_copy(slots.at[me], slot_in.at[me], slot_recv).start()
    forward_sent(0)
    forward(1)

    wait_bytes(slot_in, slot_recv)
    wait_bytes(slot_in.at[pl.ds(0, nsub - 1)], slot_send)
    slot_copy = pltpu.make_async_copy(slot_in, slot_sm, misc)
    slot_copy.start()
    inv_copy.wait()
    slot_copy.wait()

    def spread_slots(i, c):
        for u in range(4):
            s = i * 4 + u
            slot_vec[s] = jnp.where(top, slot_sm[s, 0, 0], slot_sm[s, 0, 1])
        return c

    lax.fori_loop(0, nsub // 4, spread_slots, 0)

    def iteration(k, carry):
        carry = list(carry)
        for g in range(GROUPS):
            row = sums_row(receive_forward(g), carry[g][0])
            if g > 0:
                send_far(g - 1)
            send_near(g, row)
            (forward_sent if g == 0 else return_sent)(1 - g)
            send_back(g, 1, nsub if g == 0 else CUT)

        def rest_of_return():
            send_back(1, CUT)
            send_far(1)

        carry[0] = receive_return(0, lax.rem(k, 2), *carry[0][1:], rest_of_return)
        return_sent(1)
        forward(0, 1, CUT)
        carry[1] = receive_return(1, lax.rem(k, 2), *carry[1][1:], lambda: forward(0, CUT))
        forward_sent(0)
        forward(1)
        return tuple(carry)

    one = jnp.ones(tile, jnp.float32)
    carry = lax.fori_loop(0, ITERS - 1, iteration, tuple((sums[g], one, zero) for g in range(GROUPS)))
    par = (ITERS - 1) % 2
    for g in range(GROUPS):
        send_all(g, sums_row(receive_forward(g), carry[g][0]))
        if g == 0:
            forward_sent(1)
    ends = []
    for g in range(GROUPS):
        ends.append(unfold(g, receive_all(g)))
        partner(g, par, 2).start()
    last = []
    for g in range(GROUPS):
        partner(g, par, 2).wait()
        beta, curve = steps(g, par, *ends[g], carry[g][1], carry[g][2])
        last.append((ends[g][1] / curve, beta))

    def finish(i, c):
        for u in range(UNROLL):
            p = i * UNROLL + u
            a, z = (
                sol[g, p] + last[g][0] * (res[g, p] + last[g][1] * dirn[g, p]) for g in range(GROUPS)
            )
            out[p] = jnp.where(top, a, z)
        return c

    lax.fori_loop(0, npatch // UNROLL, finish, 0)


def on_device(nsub, rhs, compliance, plate_owner, found_owner, slot_pairs, active, inverse):
    side = lax.axis_index("body")
    ncase, npatch, width = rhs.shape
    iface = inverse.shape[-1]
    nslot = iface // width
    nrow = nsub * ROOM
    owner = jnp.where(side == 0, plate_owner[:, 0], found_owner[:, 0])
    slot = jnp.where(side == 0, slot_pairs[:, 0], slot_pairs[:, 1])
    patch = jnp.arange(npatch, dtype=jnp.int32)
    same = (patch[None, :] < patch[:, None]) & (owner[None, :] == owner[:, None])
    rank = jnp.sum(same.astype(jnp.int32), axis=1)
    placed = (owner * ROOM + rank)[None, :] == jnp.arange(nrow, dtype=jnp.int32)[:, None]
    source = jnp.sum(jnp.where(placed, patch[None, :], 0), axis=1)
    sent_slot = jnp.sum(jnp.where(placed, slot[None, :] + 1, 0), axis=1) - 1
    slots = jnp.pad(sent_slot.reshape(nsub, 1, ROOM), ((0, 0), (0, 0), (0, 128 - ROOM)))

    f32, i32 = jnp.float32, jnp.int32
    vmem = pl.BlockSpec(memory_space=pltpu.VMEM)
    smem = pl.BlockSpec(memory_space=pltpu.SMEM)
    hbm = pl.BlockSpec(memory_space=pl.ANY)
    state = pltpu.VMEM((GROUPS, npatch, 8, width), f32)
    message = pltpu.VMEM((GROUPS, nsub, 8, width), f32)
    single = pltpu.VMEM((nsub, 8, width), f32)
    half = npatch // 2
    result = pl.pallas_call(
        functools.partial(kernel, nsub, npatch, nslot, width),
        out_shape=jax.ShapeDtypeStruct((npatch, ncase, width), f32),
        in_specs=[smem, smem, smem, smem, vmem, vmem, hbm, hbm],
        out_specs=vmem,
        scratch_shapes=[
            pltpu.VMEM((iface, iface), jnp.bfloat16),
            single, state, state, state, state, message, message, message, single, single,
            pltpu.VMEM((GROUPS, half + 1, 8, width), f32),
            pltpu.VMEM((2, GROUPS, half + 1, 8, width), f32),
            pltpu.VMEM((nslot, 8, width), f32),
            pltpu.VMEM((8, iface), jnp.bfloat16),
            pltpu.VMEM((nslot, 8, width), f32),
            pltpu.VMEM((nsub, 1, 128), i32),
            pltpu.SMEM((nsub, 1, 128), i32),
            pltpu.VMEM((nsub, 8, width), i32),
            pltpu.VMEM((GROUPS, 1, 128), f32),
            pltpu.VMEM((GROUPS, SPAN, 1, 128), f32),
            pltpu.VMEM((GROUPS, 1, 128), f32),
            pltpu.VMEM((GROUPS, nsub // SPAN, 1, 128), f32),
            pltpu.VMEM((GROUPS, nsub, 1, 128), f32),
            pltpu.SemaphoreType.DMA((10, GROUPS)),
            pltpu.SemaphoreType.DMA((GROUPS, 2)),
            pltpu.SemaphoreType.DMA((2, GROUPS, 2)),
            pltpu.SemaphoreType.DMA,
            pltpu.SemaphoreType.DMA,
            pltpu.SemaphoreType.DMA((8,)),
            pltpu.SemaphoreType.DMA,
            pltpu.SemaphoreType.DMA,
        ],
        compiler_params=pltpu.CompilerParams(
            collective_id=0, has_side_effects=True, vmem_limit_bytes=48 * 2**20
        ),
    )(source, owner, rank, active, compliance, slots, rhs, inverse[0, 0])
    return jnp.transpose(result, (1, 0, 2))


def solution(mesh):
    in_specs = (
        P(None, "sub", None),
        P("sub", None),
        P("sub", None),
        P("sub", None),
        P("sub", None),
        P("sub"),
        P("body", "sub", None, None),
    )
    return jax.shard_map(
        functools.partial(on_device, mesh.shape["sub"]),
        mesh=mesh, in_specs=in_specs, out_specs=P(None, "sub", None), check_vma=False,
    )
```
